256 devices in a mesh: mem: 16 (over y, x), reg: 16 (over z, core).
Axes of the slice: x: 4, y: 4, z: 8, core: 2. Of those that a mesh axis runs over, the one named last changes fastest.
Arguments:
- prior_states: bfloat16 [256, 227, 8192], P('mem', None, 'reg'), may hold values from -6 to 6
- sensor_space_runs: bfloat16 [256, 16, 8192], P('mem', 'reg'), may hold values from -6 to 6
- sensor_readings: float32 [16, 8192], P('reg'), may hold values from -8 to 8
- noise_precision: float32 [16, 8192], P('reg'), may hold values from 0.1 to 1
- reading_pointers: int32 [16, 16, 4, 512], P('reg', 'mem'), may hold values from 0 to 8703, as said below
- reading_tally: int32 [16, 16, 4], P('reg', 'mem'), may hold values from 128 to 512, as said below
Outputs:
- analysis: bfloat16 [256, 227, 8192], P('mem', None, 'reg')
The draws below stay inside these ranges and needn't reach their ends.
Inputs may be any that keep to these rules, and one draw needn't show every extreme that they name: Row reading_pointers[r, m, g, :] holds 512 distinct positions of region r's extended observations, together one window of 512 consecutive positions, in an order drawn from the seed. A local analysis uses the first reading_tally[r, m, g] entries of its list.
All inputs are finite; a program needn't handle non-finite values.
Results may differ from the reference program's by a relative error of at most 0.009.
Values may be sent and summed in bfloat16 or wider, within the bound.
No kernel may reach another device: no remote copies, remote signals or barrier semaphores. Data moves between devices by JAX's collectives and lax.ppermute only.
A program may use at most 128 MiB of HBM per device.

```python
import math
import jax
import jax.numpy as jnp
from jax import lax

RUN_AMOUNT = 256
FIELDS_PER_SITE = 227
PILLARS_PER_PATCH = 8
LMAX = 512
NOBS_R = 8192
NS_ITERS = 6
GROUPS = 4
BLOCKS = 16
REGIONS = 16
HW = 256
GRID_PILLARS = 8192


def draw_reading_pointers(key, part):
    block_total = BLOCKS * GROUPS
    positions = jnp.arange(block_total, dtype=jnp.int32)
    starts = positions * (NOBS_R + 2 * HW - LMAX) // (block_total - 1)
    keys = jax.random.split(key, REGIONS * block_total)
    orders = jax.vmap(lambda single: jax.random.permutation(single, LMAX))(keys)
    orders = orders.reshape(REGIONS, block_total, LMAX).astype(jnp.int32)
    listed = starts[None, :, None] + orders
    return listed.reshape(REGIONS, BLOCKS, GROUPS, LMAX).astype(jnp.int32)


def draw_reading_tally(key, part):
    entries = REGIONS * BLOCKS * GROUPS
    first_key, second_key = jax.random.split(key)
    counted = jax.random.randint(first_key, (entries,), LMAX // 4, LMAX + 1, dtype=jnp.int32)
    chosen = jax.random.randint(second_key, (), 0, entries, dtype=jnp.int32)
    positions = jnp.arange(entries, dtype=jnp.int32)
    counted = jnp.where(positions == chosen, LMAX, counted)
    counted = jnp.where(positions == (chosen + 1) % entries, LMAX // 4, counted)
    return counted.reshape(REGIONS, BLOCKS, GROUPS).astype(jnp.int32)


def shard_levels(rng, dims, pieces, least, top_value):
    loudness = 1.0
    for dim, parts in pieces:
        heights = jax.random.uniform(jax.random.fold_in(jax.random.fold_in(rng, 6), dim), (parts,), jnp.float32, least / len(pieces), top_value / len(pieces))
        loudness = loudness * jnp.repeat(jnp.exp(heights), dims[dim] // parts).reshape((-1,) + (1,) * (len(dims) - 1 - dim))
    return loudness


def bell_draw(stream_key, dims, spread, bound, pieces=(), kind=jnp.bfloat16):
    drawn = spread * jax.random.normal(stream_key, dims, jnp.float32)
    if pieces:
        drawn = drawn * shard_levels(stream_key, dims, pieces, -0.22, 0.18)
    return jnp.clip(drawn, -bound, bound).astype(kind)


def setup_inputs(seed: int = 0) -> dict:
    key_of = jax.random.split(jax.random.key(seed), 7)
    return {
        "prior_states": bell_draw(key_of[0], (RUN_AMOUNT, FIELDS_PER_SITE, GRID_PILLARS), 1.0, 6.0, ((0, 16), (2, 16))),
        "sensor_space_runs": bell_draw(key_of[1], (RUN_AMOUNT, REGIONS, NOBS_R), 1.0, 6.0, ((0, 16), (1, 16))),
        "sensor_readings": bell_draw(key_of[2], (REGIONS, NOBS_R), 1.5, 8.0, ((0, 16),), jnp.float32),
        "noise_precision": jnp.clip(jnp.exp(math.log(1.0) - 2.3025851 * jax.random.uniform(key_of[3], (REGIONS, NOBS_R), jnp.float32) ** shard_levels(key_of[3], (REGIONS, NOBS_R), ((0, 16),), -0.2, 0.2)), 0.1, 1.0),
        "reading_pointers": draw_reading_pointers(jax.random.fold_in(key_of[6], 71), 0),
        "reading_tally": draw_reading_tally(jax.random.fold_in(key_of[6], 71), 0),
    }


inflation = 1.1
highest = lax.Precision.HIGHEST

def nearby_correction(prior_patch, sensor_space_lines, sensor_readings, precision_nearby, pending_amount):
    runs_sequence = prior_patch.shape[0]
    prior_states_narrow = prior_patch.astype(jnp.float32)
    middle_pillar = lax.optimization_barrier(jnp.mean(prior_states_narrow, axis=0))
    deviation_matrix = (prior_states_narrow - middle_pillar[None]).astype(jnp.bfloat16)
    observed_f32 = sensor_space_lines.astype(jnp.float32)
    ens_mean = lax.optimization_barrier(jnp.mean(observed_f32, axis=0))
    anomaly = lax.optimization_barrier((observed_f32 - ens_mean[None]).astype(jnp.bfloat16)).astype(jnp.float32)
    active = (jnp.arange(sensor_space_lines.shape[1], dtype=jnp.int32) < pending_amount).astype(jnp.float32)
    weight = precision_nearby * active
    identity = jnp.eye(runs_sequence, dtype=jnp.float32)
    gram_matrix = jnp.dot(anomaly, (anomaly * weight[None, :]).T, precision=highest) + (runs_sequence - 1) / inflation * identity
    innovation_sum = jnp.dot(anomaly, weight * (sensor_readings - ens_mean), precision=highest)
    frobenius = jnp.sqrt(jnp.sum(gram_matrix * gram_matrix))
    iterate = gram_matrix / frobenius
    inverse_root = identity
    for iteration in range(NS_ITERS):
        factor = 1.5 * identity - 0.5 * jnp.dot(inverse_root, iterate, precision=highest)
        iterate = jnp.dot(iterate, factor, precision=highest)
        inverse_root = jnp.dot(factor, inverse_root, precision=highest)
    inverse_root = inverse_root / jnp.sqrt(frobenius)
    mean_weight = jnp.dot(inverse_root, jnp.dot(inverse_root, innovation_sum, precision=highest), precision=highest)
    transform = (math.sqrt(runs_sequence - 1) * inverse_root + mean_weight[:, None]).astype(jnp.bfloat16)
    combined = jnp.einsum('jvc,jk->kvc', deviation_matrix.astype(jnp.float32), transform.astype(jnp.float32), precision=highest)
    return (middle_pillar[None] + combined).astype(jnp.bfloat16)

def extend_regions(values):
    before = jnp.roll(values, 1, axis=-2)[..., -HW:]
    after = jnp.roll(values, -1, axis=-2)[..., :HW]
    return jnp.concatenate([before, values, after], axis=-1)

def reference(prior_states, sensor_space_runs, sensor_readings, noise_precision, reading_pointers, reading_tally):
    extended = extend_regions(sensor_space_runs)
    statistics = extend_regions(jnp.stack([sensor_readings, noise_precision]))
    flat_lists = reading_pointers.reshape(-1, LMAX)
    flat_counts = reading_tally.reshape(-1)
    group_total = flat_counts.shape[0]
    per_region = BLOCKS * GROUPS

    def analyse_group(patch_offset):
        region = patch_offset // per_region
        indices = lax.dynamic_index_in_dim(flat_lists, patch_offset, 0, keepdims=False)
        region_ens = lax.dynamic_index_in_dim(extended, region, 1, keepdims=False)
        sensor_space_lines = jnp.take(region_ens, indices, axis=1)
        region_stats = lax.dynamic_index_in_dim(statistics, region, 1, keepdims=False)
        chosen_moments = jnp.take(region_stats, indices, axis=1)
        prior_patch = lax.dynamic_slice_in_dim(prior_states, patch_offset * PILLARS_PER_PATCH, PILLARS_PER_PATCH, axis=2)
        pending_amount = lax.dynamic_index_in_dim(flat_counts, patch_offset, 0, keepdims=False)
        return nearby_correction(prior_patch, sensor_space_lines, chosen_moments[0], chosen_moments[1], pending_amount)
    analysed = lax.map(analyse_group, jnp.arange(group_total, dtype=jnp.int32))
    return jnp.transpose(analysed, (1, 2, 0, 3)).reshape(RUN_AMOUNT, FIELDS_PER_SITE, group_total * PILLARS_PER_PATCH)
```

```python
import functools
import math

import jax
import jax.numpy as jnp
from jax import lax
from jax.experimental import pallas as pl
from jax.experimental.pallas import tpu as pltpu
from jax.sharding import PartitionSpec as P

NS_ITERS = 6
HW = 256
LANES = 128
INFLATION = 1.1
CHUNKS = 3


def swap_blocks(tiles):
    lane = lax.broadcasted_iota(jnp.int32, tiles[0].shape, 1)
    low_half = lane < 64
    even = (lane & 32) == 0
    turned = [pltpu.roll(t, 64, 1) for t in tiles]
    first = [
        jnp.where(low_half, tiles[0], turned[2]),
        jnp.where(low_half, tiles[1], turned[3]),
        jnp.where(low_half, turned[0], tiles[2]),
        jnp.where(low_half, turned[1], tiles[3]),
    ]
    out = []
    for a, b in ((first[0], first[1]), (first[2], first[3])):
        out.append(jnp.where(even, a, pltpu.roll(b, 32, 1)))
        out.append(jnp.where(even, pltpu.roll(a, 96, 1), b))
    return out


def pack_kernel(x_ref, o_ref):
    quads = o_ref.shape[1]

    def step(t, _):
        for u in range(4):
            tiles = [
                x_ref[4 * t + i, :, u * LANES : (u + 1) * LANES].astype(jnp.float32)
                for i in range(4)
            ]
            for d, tile in enumerate(swap_blocks(tiles)):
                o_ref[4 * u + d, t] = tile.astype(jnp.bfloat16)
        return 0

    lax.fori_loop(0, quads, step, 0)


def unpack_kernel(x_ref, o_ref):
    quads = x_ref.shape[1]

    def step(t, _):
        for u in range(4):
            tiles = [x_ref[4 * u + d, t].astype(jnp.float32) for d in range(4)]
            for i, tile in enumerate(swap_blocks(tiles)):
                o_ref[4 * t + i, :, u * LANES : (u + 1) * LANES] = tile.astype(jnp.bfloat16)
        return 0

    lax.fori_loop(0, quads, step, 0)


def observe_kernel(cells_ref, left_ref, mid_ref, right_ref, o_ref, ext):
    obs = mid_ref.shape[1]
    ext[:, :HW] = left_ref[...]
    ext[:, HW : HW + obs] = mid_ref[...]
    ext[:, HW + obs : 2 * HW + obs] = right_ref[...]
    ext[:, 2 * HW + obs :] = jnp.zeros_like(ext[:, 2 * HW + obs :])
    width = o_ref.shape[3]
    for m in range(o_ref.shape[0]):
        for g in range(o_ref.shape[1]):
            first = pl.multiple_of(cells_ref[m, g] * LANES, LANES)
            o_ref[m, g] = ext[:, pl.ds(first, width)]


def halves(a):
    hi = a.astype(jnp.bfloat16)
    return hi, (a - hi.astype(jnp.float32)).astype(jnp.bfloat16)


def product(a, b):
    (ah, al), (bh, bl) = a, b
    dot = functools.partial(jnp.dot, preferred_element_type=jnp.float32)
    return dot(ah, bh) + (dot(ah, bl) + dot(al, bh))


def across(a, b):
    return lax.dot_general(a, b, (((1,), (1,)), ((), ())), preferred_element_type=jnp.float32)


def transform_kernel(
    cells_ref, tally_ref, ens_ref, ptr_ref, val_ref, inv_ref, o_ref, yh, yl, zh, zl, norm, push
):
    sources, groups, rows, width = ens_ref.shape
    members = sources * rows
    listed = ptr_ref.shape[0]
    r_i = lax.broadcasted_iota(jnp.int32, (members, members), 0)
    c_i = lax.broadcasted_iota(jnp.int32, (members, members), 1)
    eye = (r_i == c_i).astype(jnp.float32)
    place = lax.broadcasted_iota(jnp.int32, (listed, 1), 0)
    for g in range(groups):
        first = pl.multiple_of(cells_ref[g] * LANES, LANES)
        here = ptr_ref[:, g : g + 1] - first
        here = jnp.where(place < tally_ref[g], here, -1)
        spot = lax.broadcasted_iota(jnp.int32, (listed, width), 1)
        used = jnp.sum((spot == here).astype(jnp.float32), axis=0, keepdims=True)
        weight = inv_ref[:, pl.ds(first, width)] * used
        ens = ens_ref[:, g].reshape(members, width).astype(jnp.float32)
        ens_mean = jnp.sum(ens, axis=0, keepdims=True) * (1.0 / members)
        anomaly = (ens - ens_mean).astype(jnp.bfloat16)
        scaled = halves(anomaly.astype(jnp.float32) * weight)
        gram = across(anomaly, scaled[0]) + across(anomaly, scaled[1])
        gram = gram + (members - 1) / INFLATION * eye
        pull = jnp.broadcast_to(weight * (val_ref[:, pl.ds(first, width)] - ens_mean), (8, width))
        pulled = halves(pull)
        push[g] = across(pulled[0], anomaly) + across(pulled[1], anomaly)
        frobenius = jnp.sqrt(jnp.sum(gram * gram, keepdims=True))
        norm[g] = jnp.broadcast_to(1.0 / jnp.sqrt(frobenius), norm.shape[1:])
        y = gram / frobenius
        factor = 1.5 * eye - 0.5 * y
        f = halves(factor)
        zh[g], zl[g] = f
        yh[g], yl[g] = halves(product(halves(y), f))

    def step(k, _):
        for g in range(groups):
            y, z = (yh[g], yl[g]), (zh[g], zl[g])
            f = halves(1.5 * eye - 0.5 * product(z, y))
            yh[g], yl[g] = halves(product(y, f))
            zh[g], zl[g] = halves(product(f, z))
        return 0

    lax.fori_loop(1, NS_ITERS, step, 0)
    for g in range(groups):
        scale = norm[g][:1, :1]
        root = (zh[g].astype(jnp.float32) + zl[g].astype(jnp.float32)) * scale
        r = halves(root)
        moved = product(halves(product(halves(push[g]), r)), r)
        o_ref[:, g * members : (g + 1) * members] = (
            math.sqrt(members - 1) * root + moved[:1]
        ).astype(jnp.bfloat16)


def apply_kernel(t_ref, x_ref, o_ref):
    sources, quads, rows, _ = x_ref.shape
    members = sources * rows
    lane = lax.broadcasted_iota(jnp.int32, (members, LANES), 1)
    group = (lane >> 3) & 3

    def step(t, _):
        x = x_ref[:, t].reshape(members, LANES).astype(jnp.float32)
        center = jnp.sum(x, axis=0, keepdims=True) * (1.0 / members)
        pert = x - center
        stack = jnp.concatenate(
            [jnp.where(group == g, pert, 0.0).astype(jnp.bfloat16) for g in range(4)], axis=0
        )
        moved = jnp.dot(t_ref[...], stack, preferred_element_type=jnp.float32)
        o_ref[:, t] = (center + moved).astype(jnp.bfloat16).reshape(sources, rows, LANES)
        return 0

    lax.fori_loop(0, quads, step, 0)


VM = pl.BlockSpec(memory_space=pltpu.VMEM)
SM = pl.BlockSpec(memory_space=pltpu.SMEM)


def call(kernel, out_shape, in_specs, scratch=(), flops=0, size=0):
    return pl.pallas_call(
        kernel,
        out_shape=out_shape,
        in_specs=in_specs,
        out_specs=VM,
        scratch_shapes=list(scratch),
        cost_estimate=pl.CostEstimate(flops=flops, bytes_accessed=size, transcendentals=0),
        compiler_params=pltpu.CompilerParams(vmem_limit_bytes=40 << 20),
    )


def ring(count, by):
    return [(i, (i + by) % count) for i in range(count)]


def swap(a):
    return lax.all_to_all(a, "mem", split_axis=0, concat_axis=0, tiled=True)


def per_device(prior, sensor, readings, precision, pointers, tally):
    rows, fields, columns = prior.shape
    blocks = lax.axis_size("mem")
    regions = lax.axis_size("reg")
    groups = tally.shape[2]
    members = rows * blocks
    listed = pointers.shape[3]
    width = listed + LANES
    bf16, f32 = jnp.bfloat16, jnp.float32
    quads = -(-fields // 4)
    per = quads // CHUNKS

    lists = pointers[0, 0]
    cells = jnp.min(lists, axis=1) // LANES
    all_cells = swap(jnp.broadcast_to(cells[None], (blocks, groups)))

    runs = sensor[:, 0]
    obs = runs.shape[1]
    left = lax.ppermute(runs[:, obs - HW :], "reg", ring(regions, 1))
    right = lax.ppermute(runs[:, :HW], "reg", ring(regions, -1))
    stats = jnp.concatenate([readings, precision], axis=0)
    s_left = lax.ppermute(stats[:, obs - HW :], "reg", ring(regions, 1))
    s_right = lax.ppermute(stats[:, :HW], "reg", ring(regions, -1))
    stats = jnp.concatenate([s_left, stats, s_right, jnp.zeros((2, LANES), f32)], axis=1)

    by_field = jnp.transpose(prior, (1, 0, 2))
    packed = pl.pallas_call(
        pack_kernel,
        grid=(CHUNKS,),
        out_shape=jax.ShapeDtypeStruct((blocks, quads, rows, LANES), bf16),
        in_specs=[pl.BlockSpec((4 * per, rows, columns), lambda i: (i, 0, 0))],
        out_specs=pl.BlockSpec((blocks, per, rows, LANES), lambda i: (0, i, 0, 0)),
        cost_estimate=pl.CostEstimate(flops=0, bytes_accessed=2 * 2 * prior.size, transcendentals=0),
    )(by_field)

    windows = call(
        observe_kernel,
        jax.ShapeDtypeStruct((blocks, groups, rows, width), bf16),
        [SM, VM, VM, VM],
        [pltpu.VMEM((rows, obs + 2 * HW + LANES), bf16)],
        size=4 << 20,
    )(all_cells, left, runs, right)
    windows = swap(windows)
    moved = swap(packed)

    square = (groups, members, members)
    transform = call(
        transform_kernel,
        jax.ShapeDtypeStruct((members, groups * members), bf16),
        [SM, SM, VM, VM, VM, VM],
        [pltpu.VMEM(square, bf16)] * 4
        + [pltpu.VMEM((groups, 8, LANES), f32), pltpu.VMEM((groups, 8, members), f32)],
        flops=6 << 30,
        size=4 << 20,
    )(cells, tally[0, 0], windows, lists.T, stats[:1], stats[1:])

    tile = pl.BlockSpec((blocks, per, rows, LANES), lambda i: (0, i, 0, 0))
    analysed = pl.pallas_call(
        apply_kernel,
        grid=(CHUNKS,),
        out_shape=jax.ShapeDtypeStruct((blocks, quads, rows, LANES), bf16),
        in_specs=[pl.BlockSpec((members, groups * members), lambda i: (0, 0)), tile],
        out_specs=tile,
    )(transform, moved)
    back = swap(analysed)
    out = pl.pallas_call(
        unpack_kernel,
        grid=(CHUNKS,),
        out_shape=jax.ShapeDtypeStruct((fields, rows, columns), bf16),
        in_specs=[tile],
        out_specs=pl.BlockSpec((4 * per, rows, columns), lambda i: (i, 0, 0)),
    )(back)
    return jnp.transpose(out, (1, 0, 2))


def solution(mesh):
    placed = (
        P("mem", None, "reg"),
        P("mem", "reg", None),
        P("reg", None),
        P("reg", None),
        P("reg", "mem", None, None),
        P("reg", "mem", None),
    )
    return jax.shard_map(
        per_device, mesh=mesh, in_specs=placed, out_specs=P("mem", None, "reg"), check_vma=False
    )
```

```python
import functools
import math

import jax
import jax.numpy as jnp
from jax import lax
from jax.experimental import pallas as pl
from jax.experimental.pallas import tpu as pltpu
from jax.sharding import PartitionSpec as P


NS_ITERS = 6
HW = 256
EARLY = 21
LANES = 128
INFLATION = 1.1
SIDE = 4


def trade_far(a, b, low):
    turned = pltpu.roll(jnp.where(low, b, a), 64, 1)
    return jnp.where(low, a, turned), jnp.where(low, turned, b)


def trade_near(a, b, even, shift):
    turned = pltpu.roll(jnp.where(even, b, a), shift, 1)
    return jnp.where(even, a, turned), jnp.where(even, turned, b)


def lane_masks(shape):
    lane = lax.broadcasted_iota(jnp.int32, shape, 1)
    return lane < 64, (lane & 32) == 0


def spread(count, width, step):
    def some(k, _):
        for i in range(width):
            step(k * width + i)
        return 0

    lax.fori_loop(0, count // width, some, 0)
    for i in range(count - count % width, count):
        step(i)


def spans(count):
    sizes = [6] + [12] * ((count - 6) // 12)
    rest = count - sum(sizes)
    sizes += [6] * (rest // 6) + [rest % 6] * (rest % 6 > 0)
    return [(sum(sizes[:k]), n) for k, n in enumerate(sizes)]


def pack_kernel(start, x_ref, _, o_ref, held, packed, sems, out_sems):
    low, even = lane_masks(packed.shape[2:])
    quads = packed.shape[1]
    fields = min(held.shape[0], x_ref.shape[0] - 4 * start)
    pieces = spans(quads)
    copies, outs = [], []
    for c, (q, n) in enumerate(pieces):
        rows = min(4 * n, fields - 4 * q)
        copies.append(
            pltpu.make_async_copy(
                x_ref.at[pl.ds(4 * (start + q), rows)], held.at[pl.ds(4 * q, rows)], sems.at[c]
            )
        )
        outs.append(
            pltpu.make_async_copy(
                packed.at[:, pl.ds(q, n)], o_ref.at[:, pl.ds(q, n)], out_sems.at[c]
            )
        )
    for copy in copies:
        copy.start()
    for v in range(fields, 4 * quads):
        held[v] = jnp.zeros(held.shape[1:], held.dtype)

    for copy, out, (q, count) in zip(copies, outs, pieces):
        copy.wait()

        def step(t, q=q):
            t = q + t
            for u in range(4):
                a = [held[4 * t + i, :, u * LANES : (u + 1) * LANES] for i in range(4)]
                a[0], a[2] = trade_far(a[0], a[2], low)
                a[1], a[3] = trade_far(a[1], a[3], low)
                a[0], a[1] = trade_near(a[0], a[1], even, 32)
                a[2], a[3] = trade_near(a[2], a[3], even, 32)
                for d in range(4):
                    packed[4 * u + d, t] = a[d]

        spread(count, 3, step)
        out.start()
    for out in outs:
        out.wait()


def unpack_kernel(x_ref, o_ref, held, sems):
    low, even = lane_masks(x_ref.shape[2:])
    fields, quads = o_ref.shape[0], x_ref.shape[1]
    copies = []
    for c, (q, n) in enumerate(spans(quads)):
        part = pl.ds(4 * q, min(4 * n, fields - 4 * q))
        copies.append(pltpu.make_async_copy(held.at[part], o_ref.at[part], sems.at[c]))
    for copy, (first, count) in zip(copies, spans(quads)):

        def step(t, first=first):
            t = first + t
            for u in range(4):
                a = [x_ref[4 * u + d, t] for d in range(4)]
                a[0], a[1] = trade_near(a[0], a[1], even, 96)
                a[2], a[3] = trade_near(a[2], a[3], even, 96)
                a[0], a[2] = trade_far(a[0], a[2], low)
                a[1], a[3] = trade_far(a[1], a[3], low)
                for i in range(4):
                    held[4 * t + i, :, u * LANES : (u + 1) * LANES] = a[i]

        spread(count, 3, step)
        copy.start()
    for copy in copies:
        copy.wait()


def extend_kernel(left_ref, right_ref, mid_ref, val_ref, inv_ref, ext, vals, invs, _, sems):
    rows, obs = mid_ref.shape
    ends = 2 * HW + obs
    inner = pl.ds(HW, obs)
    copies = [
        pltpu.make_async_copy(ref, to.at[:, inner], sems.at[k])
        for k, (ref, to) in enumerate(((mid_ref, ext), (val_ref, vals), (inv_ref, invs)))
    ]
    for copy in copies:
        copy.start()
    for to in (ext, vals, invs):
        to[:, ends:] = jnp.zeros_like(to[:, ends:])
    for ref, first in ((left_ref, 0), (right_ref, HW + obs)):
        ext[:, first : first + HW] = ref[:rows]
        side = ref[rows:].astype(jnp.float32)
        vals[:, first : first + HW] = side[0:1] + side[2:3]
        invs[:, first : first + HW] = side[1:2] + side[3:4]
    for copy in copies:
        copy.wait()


def choose_kernel(cells_ref, *refs):
    ext_refs, o_refs = refs[:SIDE], refs[SIDE:]
    groups = cells_ref.shape[1]
    tiles = o_refs[0].shape[1] // groups
    for a, o_ref in enumerate(o_refs):
        for g in range(groups):
            first = pl.multiple_of(cells_ref[a, g] * LANES, LANES)
            for b, ext in enumerate(ext_refs):
                for k in range(tiles):
                    o_ref[b, g * tiles + k] = ext[:, pl.ds(first + k * LANES, LANES)]


def halves(a):
    hi = a.astype(jnp.bfloat16)
    return hi, (a - hi.astype(jnp.float32)).astype(jnp.bfloat16)


def product(a, b):
    (ah, al), (bh, bl) = a, b
    dot = functools.partial(jnp.dot, preferred_element_type=jnp.float32)
    return dot(ah, bh) + (dot(ah, bl) + dot(al, bh))


def across(a, b):
    return lax.dot_general(a, b, (((1,), (1,)), ((), ())), preferred_element_type=jnp.float32)


def transform_kernel(me_ref, cells_ref, tally_ref, ptr_ref, val_ref, inv_ref, *refs):
    *ens_refs, o_ref, held, yh, yl, zh, zl, norm, push = refs
    sources, tiles, rows, _ = held.shape
    groups = cells_ref.shape[0]
    tiles //= groups
    members, width = sources * rows, tiles * LANES
    y, x = me_ref[0] >> 2, me_ref[0] & 3
    for a, ens_ref in enumerate(ens_refs):
        for b in range(SIDE):
            held[((y + a) & 3) * SIDE + ((x + b) & 3)] = ens_ref[b]
    listed = ptr_ref.shape[0]
    r_i = lax.broadcasted_iota(jnp.int32, (members, members), 0)
    c_i = lax.broadcasted_iota(jnp.int32, (members, members), 1)
    eye = (r_i == c_i).astype(jnp.float32)
    place = lax.broadcasted_iota(jnp.int32, (listed, 1), 0)
    for g in range(groups):
        first = pl.multiple_of(cells_ref[g] * LANES, LANES)
        here = ptr_ref[:, g : g + 1] - first
        here = jnp.where(place < tally_ref[g], here, -1)
        spot = lax.broadcasted_iota(jnp.int32, (listed, width), 1)
        used = jnp.sum((spot == here).astype(jnp.float32), axis=0, keepdims=True)
        weight = inv_ref[:, pl.ds(first, width)] * used
        ens = jnp.concatenate(
            [held[:, g * tiles + k].reshape(members, LANES) for k in range(tiles)], axis=1
        ).astype(jnp.float32)
        ens_mean = jnp.sum(ens, axis=0, keepdims=True) * (1.0 / members)
        anomaly = (ens - ens_mean).astype(jnp.bfloat16)
        scaled = halves(anomaly.astype(jnp.float32) * weight)
        gram = across(anomaly, scaled[0]) + across(anomaly, scaled[1])
        gram = gram + (members - 1) / INFLATION * eye
        pull = jnp.broadcast_to(weight * (val_ref[:, pl.ds(first, width)] - ens_mean), (8, width))
        pulled = halves(pull)
        push[g] = across(pulled[0], anomaly) + across(pulled[1], anomaly)
        frobenius = jnp.sqrt(jnp.sum(gram * gram, keepdims=True))
        norm[g] = jnp.broadcast_to(1.0 / jnp.sqrt(frobenius), norm.shape[1:])
        y = gram / frobenius
        factor = 1.5 * eye - 0.5 * y
        f = halves(factor)
        zh[g], zl[g] = f
        yh[g], yl[g] = halves(product(halves(y), f))

    def step(k, _):
        for g in range(groups):
            y, z = (yh[g], yl[g]), (zh[g], zl[g])
            f = halves(1.5 * eye - 0.5 * product(z, y))
            yh[g], yl[g] = halves(product(y, f))
            zh[g], zl[g] = halves(product(f, z))
        return 0

    lax.fori_loop(1, NS_ITERS, step, 0)
    for g in range(groups):
        scale = norm[g][:1, :1]
        root = (zh[g].astype(jnp.float32) + zl[g].astype(jnp.float32)) * scale
        r = halves(root)
        moved = product(halves(product(halves(push[g]), r)), r)
        o_ref[:, g * members : (g + 1) * members] = (
            math.sqrt(members - 1) * root + moved[:1]
        ).astype(jnp.bfloat16)


def apply_kernel(t_ref, x_ref, *refs):
    *done_refs, o_ref, held, sems = refs
    sources, quads, rows, _ = held.shape
    place = o_ref.shape[1] - quads
    members = sources * rows
    lane = lax.broadcasted_iota(jnp.int32, (members, LANES), 1)
    group = (lane >> 3) & 3

    def some(start, count):
        centers, stacks = [], []
        for i in range(count):
            x = held[:, start + i].reshape(members, LANES).astype(jnp.float32)
            center = jnp.sum(x, axis=0, keepdims=True) * (1.0 / members)
            pert = (x - center).astype(jnp.bfloat16)
            centers.append(center)
            stacks.append(
                jnp.concatenate(
                    [jnp.where(group == g, pert, jnp.zeros_like(pert)) for g in range(4)], axis=0
                )
            )
        moved = jnp.dot(
            t_ref[...], jnp.concatenate(stacks, axis=1), preferred_element_type=jnp.float32
        )
        for i in range(count):
            part = moved[:, i * LANES : (i + 1) * LANES]
            o_ref[:, place + start + i] = (
                (centers[i] + part).astype(jnp.bfloat16).reshape(sources, rows, LANES)
            )

    copies = [
        pltpu.make_async_copy(x_ref.at[:, pl.ds(q, n)], held.at[:, pl.ds(q, n)], sems.at[c])
        for c, (q, n) in enumerate(spans(quads))
    ]
    for copy in copies:
        copy.start()
    moves = [
        pltpu.make_async_copy(ref, o_ref.at[:, pl.ds(0, place)], sems.at[len(copies)])
        for ref in done_refs
    ]
    for copy in moves:
        copy.start()
    for copy, (q, count) in zip(copies, spans(quads)):
        copy.wait()

        def step(k, _, q=q):
            some(q + k * 6, 6)
            return 0

        lax.fori_loop(0, count // 6, step, 0)
        if count % 6:
            some(q + count - count % 6, count % 6)
    for copy in moves:
        copy.wait()


VM = pl.BlockSpec(memory_space=pltpu.VMEM)
SM = pl.BlockSpec(memory_space=pltpu.SMEM)
ANY = pl.BlockSpec(memory_space=pl.ANY)
HBM = pl.BlockSpec(memory_space=pltpu.HBM)


def call(
    kernel, out_shape, in_specs, scratch=(), flops=0, size=0, limit=58, out_specs=None, aliases=None
):
    return pl.pallas_call(
        kernel,
        out_shape=out_shape,
        in_specs=in_specs,
        out_specs=jax.tree.map(lambda _: VM, out_shape) if out_specs is None else out_specs,
        scratch_shapes=list(scratch),
        input_output_aliases=aliases or {},
        cost_estimate=pl.CostEstimate(flops=flops, bytes_accessed=size, transcendentals=0),
        compiler_params=pltpu.CompilerParams(vmem_limit_bytes=limit << 20),
    )


def ring(count, by):
    return [(i, (i + by) % count) for i in range(count)]


def swap(a):
    return lax.all_to_all(a, "mem", split_axis=0, concat_axis=0, tiled=True)


def offset(a, y, x):
    pairs = [
        (((r + y) % SIDE) * SIDE + (c + x) % SIDE, r * SIDE + c)
        for r in range(SIDE)
        for c in range(SIDE)
    ]
    return lax.ppermute(a, "mem", pairs)


def per_device(prior, sensor, readings, precision, pointers, tally):
    rows, fields, columns = prior.shape
    blocks = lax.axis_size("mem")
    regions = lax.axis_size("reg")
    groups = tally.shape[2]
    members = rows * blocks
    listed = pointers.shape[3]
    width = listed + LANES
    bf16, f32, i32 = jnp.bfloat16, jnp.float32, jnp.int32
    quads = -(-fields // 4)
    shape = lambda dims, kind: jax.ShapeDtypeStruct(dims, kind)

    runs = sensor[:, 0]
    obs = runs.shape[1]
    stats = jnp.concatenate([readings, precision], axis=0)
    ends = jnp.concatenate([stats[:, :HW], stats[:, obs - HW :]], axis=1)
    coarse = ends.astype(bf16)
    fine = (ends - coarse.astype(f32)).astype(bf16)
    ends = jnp.concatenate(
        [jnp.concatenate([runs[:, :HW], runs[:, obs - HW :]], axis=1), coarse, fine], axis=0
    )
    left = lax.ppermute(ends[:, HW:], "reg", ring(regions, 1))
    right = lax.ppermute(ends[:, :HW], "reg", ring(regions, -1))

    lists = pointers[0, 0]
    cells = jnp.min(lists, axis=1) // LANES
    grid = [offset(cells, y, 0) for y in range(1, SIDE)]
    grid = jnp.stack([cells] + grid)
    me = lax.axis_index("mem").astype(i32)[None]
    reach = obs + 2 * HW + LANES
    ext, vals, invs, token = call(
        extend_kernel,
        [shape((rows, reach), bf16)] + [shape((1, reach), f32)] * 2 + [shape((8, LANES), f32)],
        [VM, VM, HBM, HBM, HBM],
        [pltpu.SemaphoreType.DMA((3,))],
        size=1 << 20,
        limit=8,
    )(left, right, runs, readings, precision)
    exts = [ext] + [offset(ext, 0, x) for x in range(1, SIDE)]

    seen = groups * width // LANES
    chosen = call(
        choose_kernel,
        [shape((SIDE, seen, rows, LANES), bf16)] * SIDE,
        [SM] + [VM] * SIDE,
        size=4 << 20,
        limit=16,
    )(grid, *exts)
    windows = [chosen[0]] + [offset(chosen[-a % SIDE], a, 0) for a in range(1, SIDE)]

    by_field = jnp.transpose(prior, (1, 0, 2))

    def pack(start, count, after):
        pieces = len(spans(count))
        return call(
            functools.partial(pack_kernel, start),
            shape((blocks, count, rows, LANES), bf16),
            [HBM, ANY],
            [
                pltpu.VMEM((4 * count, rows, columns), bf16),
                pltpu.VMEM((blocks, count, rows, LANES), bf16),
                pltpu.SemaphoreType.DMA((pieces,)),
                pltpu.SemaphoreType.DMA((pieces,)),
            ],
            size=4 * prior.size * count // quads,
            out_specs=HBM,
        )(by_field, after)

    early = pack(0, EARLY, cells)
    late = pack(EARLY, quads - EARLY, token)
    early = swap(early)
    late, early = lax.optimization_barrier((late, early))
    late = swap(late)

    square = (groups, members, members)
    transform = call(
        transform_kernel,
        shape((members, groups * members), bf16),
        [SM, SM, SM] + [VM] * (3 + SIDE),
        [pltpu.VMEM((blocks, seen, rows, LANES), bf16)]
        + [pltpu.VMEM(square, bf16)] * 4
        + [pltpu.VMEM((groups, 8, LANES), f32), pltpu.VMEM((groups, 8, members), f32)],
        flops=6 << 30,
        size=4 << 20,
        limit=24,
    )(me, cells, tally[0, 0], lists.T, vals, invs, *windows)

    def apply(states, *done):
        count = states.shape[1]
        total = count + sum(d.shape[1] for d in done)
        pieces = len(spans(count))
        return call(
            apply_kernel,
            shape((blocks, total, rows, LANES), bf16),
            [VM, ANY] + [ANY] * len(done),
            [pltpu.VMEM((blocks, count, rows, LANES), bf16), pltpu.SemaphoreType.DMA((pieces + 1,))],
            flops=(4 << 30) * count // quads,
            size=4 * prior.size * count // quads,
            limit=20,
        )(transform, states, *done)

    first = apply(early)
    analysed = apply(late, first)
    back = swap(analysed)
    out = call(
        unpack_kernel,
        shape((fields, rows, columns), bf16),
        [VM],
        [
            pltpu.VMEM((4 * quads, rows, columns), bf16),
            pltpu.SemaphoreType.DMA((len(spans(quads)),)),
        ],
        size=4 * prior.size,
        out_specs=HBM,
        limit=20,
    )(back)
    return jnp.transpose(out, (1, 0, 2))


def solution(mesh):
    placed = (
        P("mem", None, "reg"),
        P("mem", "reg", None),
        P("reg", None),
        P("reg", None),
        P("reg", "mem", None, None),
        P("reg", "mem", None),
    )
    return jax.shard_map(
        per_device, mesh=mesh, in_specs=placed, out_specs=P("mem", None, "reg"), check_vma=False
    )
```

```python
import functools
import math

import jax
import jax.numpy as jnp
from jax import lax
from jax.experimental import pallas as pl
from jax.experimental.pallas import tpu as pltpu
from jax.sharding import PartitionSpec as P


NS_ITERS = 6
HW = 256
EARLY = 18
LANES = 128
INFLATION = 1.1
SIDE = 4


def trade_far(a, b, low):
    turned = pltpu.roll(jnp.where(low, b, a), 64, 1)
    return jnp.where(low, a, turned), jnp.where(low, turned, b)


def trade_near(a, b, even, shift):
    turned = pltpu.roll(jnp.where(even, b, a), shift, 1)
    return jnp.where(even, a, turned), jnp.where(even, turned, b)


def lane_masks(shape):
    lane = lax.broadcasted_iota(jnp.int32, shape, 1)
    return lane < 64, (lane & 32) == 0


def spread(count, width, step):
    def some(k, _):
        for i in range(width):
            step(k * width + i)
        return 0

    lax.fori_loop(0, count // width, some, 0)
    for i in range(count - count % width, count):
        step(i)


def spans(count):
    sizes = [6] + [12] * ((count - 6) // 12)
    rest = count - sum(sizes)
    sizes += [6] * (rest // 6) + [rest % 6] * (rest % 6 > 0)
    return [(sum(sizes[:k]), n) for k, n in enumerate(sizes)]


def pack_kernel(start, x_ref, *refs):
    o_ref, held, packed, sems, out_sems = refs[-5:]
    low, even = lane_masks(packed.shape[2:])
    quads = packed.shape[1]
    fields = min(held.shape[0], x_ref.shape[0] - 4 * start)
    pieces = spans(quads)
    copies, outs = [], []
    for c, (q, n) in enumerate(pieces):
        rows = min(4 * n, fields - 4 * q)
        copies.append(
            pltpu.make_async_copy(
                x_ref.at[pl.ds(4 * (start + q), rows)], held.at[pl.ds(4 * q, rows)], sems.at[c]
            )
        )
        outs.append(
            pltpu.make_async_copy(
                packed.at[:, pl.ds(q, n)], o_ref.at[:, pl.ds(start + q, n)], out_sems.at[c]
            )
        )
    for copy in copies:
        copy.start()
    for v in range(fields, 4 * quads):
        held[v] = jnp.zeros(held.shape[1:], held.dtype)

    for copy, out, (q, count) in zip(copies, outs, pieces):
        copy.wait()

        def step(t, q=q):
            t = q + t
            for u in range(4):
                a = [held[4 * t + i, :, u * LANES : (u + 1) * LANES] for i in range(4)]
                a[0], a[2] = trade_far(a[0], a[2], low)
                a[1], a[3] = trade_far(a[1], a[3], low)
                a[0], a[1] = trade_near(a[0], a[1], even, 32)
                a[2], a[3] = trade_near(a[2], a[3], even, 32)
                for d in range(4):
                    packed[4 * u + d, t] = a[d]

        spread(count, 3, step)
        out.start()
    for out in outs:
        out.wait()


def unpack_kernel(x_ref, o_ref, held, sems):
    low, even = lane_masks(x_ref.shape[2:])
    fields, quads = o_ref.shape[0], x_ref.shape[1]
    copies = []
    for c, (q, n) in enumerate(spans(quads)):
        part = pl.ds(4 * q, min(4 * n, fields - 4 * q))
        copies.append(pltpu.make_async_copy(held.at[part], o_ref.at[part], sems.at[c]))
    for copy, (first, count) in zip(copies, spans(quads)):

        def step(t, first=first):
            t = first + t
            for u in range(4):
                a = [x_ref[4 * u + d, t] for d in range(4)]
                a[0], a[1] = trade_near(a[0], a[1], even, 96)
                a[2], a[3] = trade_near(a[2], a[3], even, 96)
                a[0], a[2] = trade_far(a[0], a[2], low)
                a[1], a[3] = trade_far(a[1], a[3], low)
                for i in range(4):
                    held[4 * t + i, :, u * LANES : (u + 1) * LANES] = a[i]

        spread(count, 3, step)
        copy.start()
    for copy in copies:
        copy.wait()


def choose_kernel(
    cells_ref, left_ref, right_ref, val_ref, inv_ref, mid_ref, *refs
):
    runs_refs, side_refs = refs[: SIDE - 1], refs[SIDE - 1 : 2 * SIDE - 2]
    *o_refs, vals, invs, ext, sems = refs[2 * SIDE - 2 :]
    rows, obs = mid_ref.shape
    ends = 2 * HW + obs
    inner = pl.ds(HW, obs)
    copies = [
        pltpu.make_async_copy(ref, to.at[:, inner], sems.at[k])
        for k, (ref, to) in enumerate(((mid_ref, ext.at[0]), (val_ref, vals), (inv_ref, invs)))
    ]
    for copy in copies:
        copy.start()
    for to in (vals, invs):
        to[:, ends:] = jnp.zeros_like(to[:, ends:])
    for ref, first in ((left_ref, 0), (right_ref, HW + obs)):
        ext[0, :, first : first + HW] = ref[:rows]
        side = ref[rows:].astype(jnp.float32)
        vals[:, first : first + HW] = side[0:1] + side[2:3]
        invs[:, first : first + HW] = side[1:2] + side[3:4]
    for b in range(SIDE):
        ext[b, :, ends:] = jnp.zeros_like(ext[b, :, ends:])
    for b, (ref, sides) in enumerate(zip(runs_refs, side_refs)):
        ext[b + 1, :, :HW] = sides[:, :HW]
        ext[b + 1, :, HW : HW + obs] = ref[...]
        ext[b + 1, :, HW + obs : ends] = sides[:, HW:]
    for copy in copies:
        copy.wait()
    groups = cells_ref.shape[1]
    tiles = o_refs[0].shape[1] // groups
    for a, o_ref in enumerate(o_refs):
        for g in range(groups):
            first = pl.multiple_of(cells_ref[a, g] * LANES, LANES)
            for b in range(SIDE):
                for k in range(tiles):
                    o_ref[b, g * tiles + k] = ext[b, :, pl.ds(first + k * LANES, LANES)]


def halves(a):
    hi = a.astype(jnp.bfloat16)
    return hi, (a - hi.astype(jnp.float32)).astype(jnp.bfloat16)


def product(a, b):
    (ah, al), (bh, bl) = a, b
    dot = functools.partial(jnp.dot, preferred_element_type=jnp.float32)
    return dot(ah, bh) + (dot(ah, bl) + dot(al, bh))


def across(a, b):
    return lax.dot_general(a, b, (((1,), (1,)), ((), ())), preferred_element_type=jnp.float32)


def transform_kernel(me_ref, cells_ref, tally_ref, ptr_ref, val_ref, inv_ref, *refs):
    *ens_refs, o_ref, held, yh, yl, zh, zl, norm, push = refs
    sources, tiles, rows, _ = held.shape
    groups = cells_ref.shape[0]
    tiles //= groups
    members, width = sources * rows, tiles * LANES
    y, x = me_ref[0] >> 2, me_ref[0] & 3
    for a, ens_ref in enumerate(ens_refs):
        for b in range(SIDE):
            held[((y + a) & 3) * SIDE + ((x + b) & 3)] = ens_ref[b]
    listed = ptr_ref.shape[0]
    r_i = lax.broadcasted_iota(jnp.int32, (members, members), 0)
    c_i = lax.broadcasted_iota(jnp.int32, (members, members), 1)
    eye = (r_i == c_i).astype(jnp.float32)
    place = lax.broadcasted_iota(jnp.int32, (listed, 1), 0)
    for g in range(groups):
        first = pl.multiple_of(cells_ref[g] * LANES, LANES)
        here = ptr_ref[:, g : g + 1] - first
        here = jnp.where(place < tally_ref[g], here, -1)
        spot = lax.broadcasted_iota(jnp.int32, (listed, width), 1)
        used = jnp.sum((spot == here).astype(jnp.float32), axis=0, keepdims=True)
        weight = inv_ref[:, pl.ds(first, width)] * used
        ens = jnp.concatenate(
            [held[:, g * tiles + k].reshape(members, LANES) for k in range(tiles)], axis=1
        ).astype(jnp.float32)
        ens_mean = jnp.sum(ens, axis=0, keepdims=True) * (1.0 / members)
        anomaly = (ens - ens_mean).astype(jnp.bfloat16)
        scaled = halves(anomaly.astype(jnp.float32) * weight)
        gram = across(anomaly, scaled[0]) + across(anomaly, scaled[1])
        gram = gram + (members - 1) / INFLATION * eye
        pull = jnp.broadcast_to(weight * (val_ref[:, pl.ds(first, width)] - ens_mean), (8, width))
        pulled = halves(pull)
        push[g] = across(pulled[0], anomaly) + across(pulled[1], anomaly)
        frobenius = jnp.sqrt(jnp.sum(gram * gram, keepdims=True))
        norm[g] = jnp.broadcast_to(1.0 / jnp.sqrt(frobenius), norm.shape[1:])
        y = gram / frobenius
        factor = 1.5 * eye - 0.5 * y
        f = halves(factor)
        zh[g], zl[g] = f
        yh[g], yl[g] = halves(product(halves(y), f))

    def step(k, _):
        for g in range(groups):
            y, z = (yh[g], yl[g]), (zh[g], zl[g])
            f = halves(1.5 * eye - 0.5 * product(z, y))
            yh[g], yl[g] = halves(product(y, f))
            zh[g], zl[g] = halves(product(f, z))
        return 0

    lax.fori_loop(1, NS_ITERS, step, 0)
    for g in range(groups):
        scale = norm[g][:1, :1]
        root = (zh[g].astype(jnp.float32) + zl[g].astype(jnp.float32)) * scale
        r = halves(root)
        moved = product(halves(product(halves(push[g]), r)), r)
        o_ref[:, g * members : (g + 1) * members] = (
            math.sqrt(members - 1) * root + moved[:1]
        ).astype(jnp.bfloat16)


def apply_kernel(t_ref, x_ref, o_ref, held, sems):
    sources, quads, rows, _ = held.shape
    members = sources * rows
    lane = lax.broadcasted_iota(jnp.int32, (members, LANES), 1)
    group = (lane >> 3) & 3

    def some(start, count):
        centers, stacks = [], []
        for i in range(count):
            x = held[:, start + i].reshape(members, LANES).astype(jnp.float32)
            center = jnp.sum(x, axis=0, keepdims=True) * (1.0 / members)
            pert = (x - center).astype(jnp.bfloat16)
            centers.append(center)
            stacks.append(
                jnp.concatenate(
                    [jnp.where(group == g, pert, jnp.zeros_like(pert)) for g in range(4)], axis=0
                )
            )
        moved = jnp.dot(
            t_ref[...], jnp.concatenate(stacks, axis=1), preferred_element_type=jnp.float32
        )
        for i in range(count):
            part = moved[:, i * LANES : (i + 1) * LANES]
            o_ref[:, start + i] = (
                (centers[i] + part).astype(jnp.bfloat16).reshape(sources, rows, LANES)
            )

    pieces = spans(quads)
    copies = [
        pltpu.make_async_copy(x_ref.at[:, pl.ds(q, n)], held.at[:, pl.ds(q, n)], sems.at[c])
        for c, (q, n) in enumerate(pieces)
    ]
    for copy in copies:
        copy.start()
    for copy, (q, count) in zip(copies, pieces):
        copy.wait()

        def step(k, _, q=q):
            some(q + k * 6, 6)
            return 0

        lax.fori_loop(0, count // 6, step, 0)
        if count % 6:
            some(q + count - count % 6, count % 6)


VM = pl.BlockSpec(memory_space=pltpu.VMEM)
SM = pl.BlockSpec(memory_space=pltpu.SMEM)
ANY = pl.BlockSpec(memory_space=pl.ANY)
HBM = pl.BlockSpec(memory_space=pltpu.HBM)


def call(
    kernel, out_shape, in_specs, scratch=(), flops=0, size=0, limit=58, out_specs=None, aliases=None
):
    return pl.pallas_call(
        kernel,
        out_shape=out_shape,
        in_specs=in_specs,
        out_specs=jax.tree.map(lambda _: VM, out_shape) if out_specs is None else out_specs,
        scratch_shapes=list(scratch),
        input_output_aliases=aliases or {},
        cost_estimate=pl.CostEstimate(flops=flops, bytes_accessed=size, transcendentals=0),
        compiler_params=pltpu.CompilerParams(vmem_limit_bytes=int(limit * (1 << 20))),
    )


def ring(count, by):
    return [(i, (i + by) % count) for i in range(count)]


def swap(a):
    return lax.all_to_all(a, "mem", split_axis=0, concat_axis=0, tiled=True)


def offset(a, y, x):
    pairs = [
        (((r + y) % SIDE) * SIDE + (c + x) % SIDE, r * SIDE + c)
        for r in range(SIDE)
        for c in range(SIDE)
    ]
    return lax.ppermute(a, "mem", pairs)


def per_device(prior, sensor, readings, precision, pointers, tally):
    rows, fields, columns = prior.shape
    blocks = lax.axis_size("mem")
    regions = lax.axis_size("reg")
    groups = tally.shape[2]
    members = rows * blocks
    listed = pointers.shape[3]
    width = listed + LANES
    bf16, f32, i32 = jnp.bfloat16, jnp.float32, jnp.int32
    quads = -(-fields // 4)
    shape = lambda dims, kind: jax.ShapeDtypeStruct(dims, kind)

    runs = sensor[:, 0]
    obs = runs.shape[1]
    stats = jnp.concatenate([readings, precision], axis=0)
    ends = jnp.concatenate([stats[:, :HW], stats[:, obs - HW :]], axis=1)
    coarse = ends.astype(bf16)
    fine = (ends - coarse.astype(f32)).astype(bf16)
    ends = jnp.concatenate(
        [jnp.concatenate([runs[:, :HW], runs[:, obs - HW :]], axis=1), coarse, fine], axis=0
    )
    left = lax.ppermute(ends[:, HW:], "reg", ring(regions, 1))
    right = lax.ppermute(ends[:, :HW], "reg", ring(regions, -1))

    lists = pointers[0, 0]
    cells = jnp.min(lists, axis=1) // LANES
    grid = [offset(cells, y, 0) for y in range(1, SIDE)]
    grid = jnp.stack([cells] + grid)
    me = lax.axis_index("mem").astype(i32)[None]
    reach = obs + 2 * HW + LANES
    others = [offset(runs, 0, x) for x in range(1, SIDE)]
    sides = jnp.concatenate([left[:rows], right[:rows]], axis=1)
    sides = [offset(sides, 0, x) for x in range(1, SIDE)]

    seen = groups * width // LANES
    *chosen, vals, invs = call(
        choose_kernel,
        [shape((SIDE, seen, rows, LANES), bf16)] * SIDE + [shape((1, reach), f32)] * 2,
        [SM, VM, VM, HBM, HBM, HBM] + [VM] * (2 * SIDE - 2),
        [pltpu.VMEM((SIDE, rows, reach), bf16), pltpu.SemaphoreType.DMA((3,))],
        size=4 << 20,
        limit=16,
    )(grid, left, right, readings, precision, runs, *others, *sides)
    windows = [chosen[0]] + [offset(chosen[-a % SIDE], a, 0) for a in range(1, SIDE)]

    by_field = jnp.transpose(prior, (1, 0, 2))

    def pack(start, count, *into):
        pieces = len(spans(count))
        return call(
            functools.partial(pack_kernel, start),
            shape((blocks, quads, rows, LANES), bf16),
            [HBM] + [HBM] * len(into),
            [
                pltpu.VMEM((4 * count, rows, columns), bf16),
                pltpu.VMEM((blocks, count, rows, LANES), bf16),
                pltpu.SemaphoreType.DMA((pieces,)),
                pltpu.SemaphoreType.DMA((pieces,)),
            ],
            size=4 * prior.size * count // quads,
            out_specs=HBM,
            aliases={1: 0} if into else None,
        )(by_field, *into)

    packed = pack(0, EARLY)
    packed = pack(EARLY, quads - EARLY, packed)
    moved = swap(packed)

    square = (groups, members, members)
    transform = call(
        transform_kernel,
        shape((members, groups * members), bf16),
        [SM, SM, SM] + [VM] * (3 + SIDE),
        [pltpu.VMEM((blocks, seen, rows, LANES), bf16)]
        + [pltpu.VMEM(square, bf16)] * 4
        + [pltpu.VMEM((groups, 8, LANES), f32), pltpu.VMEM((groups, 8, members), f32)],
        flops=6 << 30,
        size=4 << 20,
        limit=24,
    )(me, cells, tally[0, 0], lists.T, vals, invs, *windows)

    analysed = call(
        apply_kernel,
        shape((blocks, quads, rows, LANES), bf16),
        [VM, HBM],
        [
            pltpu.VMEM((blocks, quads, rows, LANES), bf16),
            pltpu.SemaphoreType.DMA((len(spans(quads)),)),
        ],
        flops=4 << 30,
        size=4 * prior.size,
        limit=20,
    )(transform, moved)
    back = swap(analysed)
    out = call(
        unpack_kernel,
        shape((fields, rows, columns), bf16),
        [VM],
        [
            pltpu.VMEM((4 * quads, rows, columns), bf16),
            pltpu.SemaphoreType.DMA((len(spans(quads)),)),
        ],
        size=4 * prior.size,
        out_specs=HBM,
        limit=20,
    )(back)
    return jnp.transpose(out, (1, 0, 2))


def solution(mesh):
    placed = (
        P("mem", None, "reg"),
        P("mem", "reg", None),
        P("reg", None),
        P("reg", None),
        P("reg", "mem", None, None),
        P("reg", "mem", None),
    )
    return jax.shard_map(
        per_device, mesh=mesh, in_specs=placed, out_specs=P("mem", None, "reg"), check_vma=False
    )
```

```python
import functools
import math

import jax
import jax.numpy as jnp
from jax import lax
from jax.experimental import pallas as pl
from jax.experimental.pallas import tpu as pltpu
from jax.sharding import PartitionSpec as P


NS_ITERS = 6
HW = 256
EARLY = 18
LANES = 128
INFLATION = 1.1
SIDE = 4


def trade_far(a, b, low):
    turned = pltpu.roll(jnp.where(low, b, a), 64, 1)
    return jnp.where(low, a, turned), jnp.where(low, turned, b)


def trade_near(a, b, even, shift):
    turned = pltpu.roll(jnp.where(even, b, a), shift, 1)
    return jnp.where(even, a, turned), jnp.where(even, turned, b)


def lane_masks(shape):
    lane = lax.broadcasted_iota(jnp.int32, shape, 1)
    return lane < 64, (lane & 32) == 0


def spread(count, width, step):
    def some(k, _):
        for i in range(width):
            step(k * width + i)
        return 0

    lax.fori_loop(0, count // width, some, 0)
    for i in range(count - count % width, count):
        step(i)


def spans(count):
    sizes = [6] + [12] * ((count - 6) // 12)
    rest = count - sum(sizes)
    sizes += [6] * (rest // 6) + [rest % 6] * (rest % 6 > 0)
    return [(sum(sizes[:k]), n) for k, n in enumerate(sizes)]


def pack_kernel(start, x_ref, *refs):
    o_ref, held, packed, sems, out_sems = refs[-5:]
    low, even = lane_masks(packed.shape[2:])
    quads = packed.shape[1]
    fields = min(held.shape[0], x_ref.shape[0] - 4 * start)
    pieces = spans(quads)
    copies, outs = [], []
    for c, (q, n) in enumerate(pieces):
        rows = min(4 * n, fields - 4 * q)
        copies.append(
            pltpu.make_async_copy(
                x_ref.at[pl.ds(4 * (start + q), rows)], held.at[pl.ds(4 * q, rows)], sems.at[c]
            )
        )
        outs.append(
            pltpu.make_async_copy(
                packed.at[:, pl.ds(q, n)], o_ref.at[:, pl.ds(start + q, n)], out_sems.at[c]
            )
        )
    for copy in copies:
        copy.start()
    for v in range(fields, 4 * quads):
        held[v] = jnp.zeros(held.shape[1:], held.dtype)

    for copy, out, (q, count) in zip(copies, outs, pieces):
        copy.wait()

        def step(t, q=q):
            t = q + t
            for u in range(4):
                a = [held[4 * t + i, :, u * LANES : (u + 1) * LANES] for i in range(4)]
                a[0], a[2] = trade_far(a[0], a[2], low)
                a[1], a[3] = trade_far(a[1], a[3], low)
                a[0], a[1] = trade_near(a[0], a[1], even, 32)
                a[2], a[3] = trade_near(a[2], a[3], even, 32)
                for d in range(4):
                    packed[4 * u + d, t] = a[d]

        spread(count, 3, step)
        out.start()
    for out in outs:
        out.wait()


def unpack_kernel(x_ref, o_ref, held, sems):
    low, even = lane_masks(x_ref.shape[2:])
    fields, quads = o_ref.shape[0], x_ref.shape[1]
    copies = []
    for c, (q, n) in enumerate(spans(quads)):
        part = pl.ds(4 * q, min(4 * n, fields - 4 * q))
        copies.append(pltpu.make_async_copy(held.at[part], o_ref.at[part], sems.at[c]))
    for copy, (first, count) in zip(copies, spans(quads)):

        def step(t, first=first):
            t = first + t
            for u in range(4):
                a = [x_ref[4 * u + d, t] for d in range(4)]
                a[0], a[1] = trade_near(a[0], a[1], even, 96)
                a[2], a[3] = trade_near(a[2], a[3], even, 96)
                a[0], a[2] = trade_far(a[0], a[2], low)
                a[1], a[3] = trade_far(a[1], a[3], low)
                for i in range(4):
                    held[4 * t + i, :, u * LANES : (u + 1) * LANES] = a[i]

        spread(count, 3, step)
        copy.start()
    for copy in copies:
        copy.wait()


def edges_kernel(runs_ref, val_ref, inv_ref, lists_ref, head_ref, tail_ref, cells_ref, ends, sems):
    _, obs = runs_ref.shape
    copies = [
        pltpu.make_async_copy(runs_ref.at[:, pl.ds(first, HW)], ends.at[k], sems.at[k])
        for k, first in enumerate((0, obs - HW))
    ]
    for copy in copies:
        copy.start()
    for g in range(lists_ref.shape[2]):
        cells_ref[g] = jnp.min(lists_ref[0, 0, g : g + 1]) >> 7
    for k, (ref, first) in enumerate(((head_ref, 0), (tail_ref, obs - HW))):
        part = jnp.concatenate([val_ref[:, first : first + HW], inv_ref[:, first : first + HW]])
        coarse = part.astype(jnp.bfloat16)
        fine = part - coarse.astype(jnp.float32)
        side = jnp.concatenate([coarse.astype(jnp.float32), fine], axis=0)
        copies[k].wait()
        ref[...] = jnp.concatenate([ends[k].astype(jnp.float32), side]).astype(jnp.bfloat16)


def choose_kernel(
    cells_ref, left_ref, right_ref, val_ref, inv_ref, mid_ref, *refs
):
    runs_refs, side_refs = refs[: SIDE - 1], refs[SIDE - 1 : 2 * SIDE - 2]
    *o_refs, vals, invs, ext, sems = refs[2 * SIDE - 2 :]
    rows, obs = mid_ref.shape
    ends = 2 * HW + obs
    inner = pl.ds(HW, obs)
    copies = [
        pltpu.make_async_copy(ref, to.at[:, inner], sems.at[k])
        for k, (ref, to) in enumerate(((mid_ref, ext.at[0]), (val_ref, vals), (inv_ref, invs)))
    ]
    for copy in copies:
        copy.start()
    for to in (vals, invs):
        to[:, ends:] = jnp.zeros_like(to[:, ends:])
    for ref, first in ((left_ref, 0), (right_ref, HW + obs)):
        ext[0, :, first : first + HW] = ref[:rows]
        side = ref[rows:].astype(jnp.float32)
        vals[:, first : first + HW] = side[0:1] + side[2:3]
        invs[:, first : first + HW] = side[1:2] + side[3:4]
    for b in range(SIDE):
        ext[b, :, ends:] = jnp.zeros_like(ext[b, :, ends:])
    for b, (ref, sides) in enumerate(zip(runs_refs, side_refs)):
        ext[b + 1, :, :HW] = sides[:, :HW]
        ext[b + 1, :, HW : HW + obs] = ref[...]
        ext[b + 1, :, HW + obs : ends] = sides[:, HW:]
    for copy in copies:
        copy.wait()
    groups = cells_ref.shape[1]
    tiles = o_refs[0].shape[1] // groups
    for a, o_ref in enumerate(o_refs):
        for g in range(groups):
            first = pl.multiple_of(cells_ref[a, g] * LANES, LANES)
            for b in range(SIDE):
                for k in range(tiles):
                    o_ref[b, g * tiles + k] = ext[b, :, pl.ds(first + k * LANES, LANES)]


def halves(a):
    hi = a.astype(jnp.bfloat16)
    return hi, (a - hi.astype(jnp.float32)).astype(jnp.bfloat16)


def product(a, b):
    (ah, al), (bh, bl) = a, b
    dot = functools.partial(jnp.dot, preferred_element_type=jnp.float32)
    return dot(ah, bh) + (dot(ah, bl) + dot(al, bh))


def across(a, b):
    return lax.dot_general(a, b, (((1,), (1,)), ((), ())), preferred_element_type=jnp.float32)


def transform_kernel(me_ref, cells_ref, tally_ref, ptr_ref, val_ref, inv_ref, *refs):
    *ens_refs, o_ref, held, yh, yl, zh, zl, norm, push = refs
    sources, tiles, rows, _ = held.shape
    groups = cells_ref.shape[0]
    tiles //= groups
    members, width = sources * rows, tiles * LANES
    y, x = me_ref[0] >> 2, me_ref[0] & 3
    for a, ens_ref in enumerate(ens_refs):
        for b in range(SIDE):
            held[((y + a) & 3) * SIDE + ((x + b) & 3)] = ens_ref[b]
    listed = ptr_ref.shape[0]
    r_i = lax.broadcasted_iota(jnp.int32, (members, members), 0)
    c_i = lax.broadcasted_iota(jnp.int32, (members, members), 1)
    eye = (r_i == c_i).astype(jnp.float32)
    place = lax.broadcasted_iota(jnp.int32, (listed, 1), 0)
    for g in range(groups):
        first = pl.multiple_of(cells_ref[g] * LANES, LANES)
        here = ptr_ref[:, g : g + 1] - first
        here = jnp.where(place < tally_ref[g], here, -1)
        spot = lax.broadcasted_iota(jnp.int32, (listed, width), 1)
        used = jnp.sum((spot == here).astype(jnp.float32), axis=0, keepdims=True)
        weight = inv_ref[:, pl.ds(first, width)] * used
        ens = jnp.concatenate(
            [held[:, g * tiles + k].reshape(members, LANES) for k in range(tiles)], axis=1
        ).astype(jnp.float32)
        ens_mean = jnp.sum(ens, axis=0, keepdims=True) * (1.0 / members)
        anomaly = (ens - ens_mean).astype(jnp.bfloat16)
        scaled = halves(anomaly.astype(jnp.float32) * weight)
        gram = across(anomaly, scaled[0]) + across(anomaly, scaled[1])
        gram = gram + (members - 1) / INFLATION * eye
        pull = jnp.broadcast_to(weight * (val_ref[:, pl.ds(first, width)] - ens_mean), (8, width))
        pulled = halves(pull)
        push[g] = across(pulled[0], anomaly) + across(pulled[1], anomaly)
        frobenius = jnp.sqrt(jnp.sum(gram * gram, keepdims=True))
        norm[g] = jnp.broadcast_to(1.0 / jnp.sqrt(frobenius), norm.shape[1:])
        y = gram / frobenius
        factor = 1.5 * eye - 0.5 * y
        f = halves(factor)
        zh[g], zl[g] = f
        yh[g], yl[g] = halves(product(halves(y), f))

    def step(k, _):
        for g in range(groups):
            y, z = (yh[g], yl[g]), (zh[g], zl[g])
            f = halves(1.5 * eye - 0.5 * product(z, y))
            yh[g], yl[g] = halves(product(y, f))
            zh[g], zl[g] = halves(product(f, z))
        return 0

    lax.fori_loop(1, NS_ITERS, step, 0)
    for g in range(groups):
        scale = norm[g][:1, :1]
        root = (zh[g].astype(jnp.float32) + zl[g].astype(jnp.float32)) * scale
        r = halves(root)
        moved = product(halves(product(halves(push[g]), r)), r)
        o_ref[:, g * members : (g + 1) * members] = (
            math.sqrt(members - 1) * root + moved[:1]
        ).astype(jnp.bfloat16)


def apply_kernel(t_ref, x_ref, o_ref, held, sems):
    sources, quads, rows, _ = held.shape
    members = sources * rows
    lane = lax.broadcasted_iota(jnp.int32, (members, LANES), 1)
    group = (lane >> 3) & 3

    def some(start, count):
        centers, stacks = [], []
        for i in range(count):
            x = held[:, start + i].reshape(members, LANES).astype(jnp.float32)
            center = jnp.sum(x, axis=0, keepdims=True) * (1.0 / members)
            pert = (x - center).astype(jnp.bfloat16)
            centers.append(center)
            stacks.append(
                jnp.concatenate(
                    [jnp.where(group == g, pert, jnp.zeros_like(pert)) for g in range(4)], axis=0
                )
            )
        moved = jnp.dot(
            t_ref[...], jnp.concatenate(stacks, axis=1), preferred_element_type=jnp.float32
        )
        for i in range(count):
            part = moved[:, i * LANES : (i + 1) * LANES]
            o_ref[:, start + i] = (
                (centers[i] + part).astype(jnp.bfloat16).reshape(sources, rows, LANES)
            )

    pieces = spans(quads)
    copies = [
        pltpu.make_async_copy(x_ref.at[:, pl.ds(q, n)], held.at[:, pl.ds(q, n)], sems.at[c])
        for c, (q, n) in enumerate(pieces)
    ]
    for copy in copies:
        copy.start()
    for copy, (q, count) in zip(copies, pieces):
        copy.wait()

        def step(k, _, q=q):
            some(q + k * 6, 6)
            return 0

        lax.fori_loop(0, count // 6, step, 0)
        if count % 6:
            some(q + count - count % 6, count % 6)


VM = pl.BlockSpec(memory_space=pltpu.VMEM)
SM = pl.BlockSpec(memory_space=pltpu.SMEM)
ANY = pl.BlockSpec(memory_space=pl.ANY)
HBM = pl.BlockSpec(memory_space=pltpu.HBM)


def call(
    kernel, out_shape, in_specs, scratch=(), flops=0, size=0, limit=58, out_specs=None, aliases=None
):
    return pl.pallas_call(
        kernel,
        out_shape=out_shape,
        in_specs=in_specs,
        out_specs=jax.tree.map(lambda _: VM, out_shape) if out_specs is None else out_specs,
        scratch_shapes=list(scratch),
        input_output_aliases=aliases or {},
        cost_estimate=pl.CostEstimate(flops=flops, bytes_accessed=size, transcendentals=0),
        compiler_params=pltpu.CompilerParams(vmem_limit_bytes=int(limit * (1 << 20))),
    )


def ring(count, by):
    return [(i, (i + by) % count) for i in range(count)]


def swap(a):
    return lax.all_to_all(a, "mem", split_axis=0, concat_axis=0, tiled=True)


def offset(a, y, x):
    pairs = [
        (((r + y) % SIDE) * SIDE + (c + x) % SIDE, r * SIDE + c)
        for r in range(SIDE)
        for c in range(SIDE)
    ]
    return lax.ppermute(a, "mem", pairs)


def per_device(prior, sensor, readings, precision, pointers, tally):
    rows, fields, columns = prior.shape
    blocks = lax.axis_size("mem")
    regions = lax.axis_size("reg")
    groups = tally.shape[2]
    members = rows * blocks
    listed = pointers.shape[3]
    width = listed + LANES
    bf16, f32, i32 = jnp.bfloat16, jnp.float32, jnp.int32
    quads = -(-fields // 4)
    shape = lambda dims, kind: jax.ShapeDtypeStruct(dims, kind)

    runs = sensor[:, 0]
    obs = runs.shape[1]
    lists = pointers[0, 0]
    head, tail, cells = call(
        edges_kernel,
        [shape((rows + 4, HW), bf16)] * 2 + [shape((groups,), i32)],
        [HBM, VM, VM, VM],
        [pltpu.VMEM((2, rows, HW), bf16), pltpu.SemaphoreType.DMA((2,))],
        size=1 << 16,
        limit=63.89,
        out_specs=[VM, VM, SM],
    )(runs, readings, precision, pointers)
    left = lax.ppermute(tail, "reg", ring(regions, 1))
    right = lax.ppermute(head, "reg", ring(regions, -1))

    grid = [offset(cells, y, 0) for y in range(1, SIDE)]
    grid = jnp.stack([cells] + grid)
    me = lax.axis_index("mem").astype(i32)[None]
    reach = obs + 2 * HW + LANES
    others = [offset(runs, 0, x) for x in range(1, SIDE)]
    sides = jnp.concatenate([left[:rows], right[:rows]], axis=1)
    sides = [offset(sides, 0, x) for x in range(1, SIDE)]

    seen = groups * width // LANES
    *chosen, vals, invs = call(
        choose_kernel,
        [shape((SIDE, seen, rows, LANES), bf16)] * SIDE + [shape((1, reach), f32)] * 2,
        [SM, VM, VM, HBM, HBM, HBM] + [VM] * (2 * SIDE - 2),
        [pltpu.VMEM((SIDE, rows, reach), bf16), pltpu.SemaphoreType.DMA((3,))],
        size=4 << 20,
        limit=16,
    )(grid, left, right, readings, precision, runs, *others, *sides)
    windows = [chosen[0]] + [offset(chosen[-a % SIDE], a, 0) for a in range(1, SIDE)]

    by_field = jnp.transpose(prior, (1, 0, 2))

    def pack(start, count, *into):
        pieces = len(spans(count))
        return call(
            functools.partial(pack_kernel, start),
            shape((blocks, quads, rows, LANES), bf16),
            [HBM] + [HBM] * len(into),
            [
                pltpu.VMEM((4 * count, rows, columns), bf16),
                pltpu.VMEM((blocks, count, rows, LANES), bf16),
                pltpu.SemaphoreType.DMA((pieces,)),
                pltpu.SemaphoreType.DMA((pieces,)),
            ],
            size=4 * prior.size * count // quads,
            out_specs=HBM,
            aliases={1: 0} if into else None,
        )(by_field, *into)

    packed = pack(0, EARLY)
    packed = pack(EARLY, quads - EARLY, packed)
    moved = swap(packed)

    square = (groups, members, members)
    transform = call(
        transform_kernel,
        shape((members, groups * members), bf16),
        [SM, SM, SM] + [VM] * (3 + SIDE),
        [pltpu.VMEM((blocks, seen, rows, LANES), bf16)]
        + [pltpu.VMEM(square, bf16)] * 4
        + [pltpu.VMEM((groups, 8, LANES), f32), pltpu.VMEM((groups, 8, members), f32)],
        flops=6 << 30,
        size=4 << 20,
        limit=24,
    )(me, cells, tally[0, 0], lists.T, vals, invs, *windows)

    analysed = call(
        apply_kernel,
        shape((blocks, quads, rows, LANES), bf16),
        [VM, HBM],
        [
            pltpu.VMEM((blocks, quads, rows, LANES), bf16),
            pltpu.SemaphoreType.DMA((len(spans(quads)),)),
        ],
        flops=4 << 30,
        size=4 * prior.size,
        limit=20,
    )(transform, moved)
    back = swap(analysed)
    out = call(
        unpack_kernel,
        shape((fields, rows, columns), bf16),
        [VM],
        [
            pltpu.VMEM((4 * quads, rows, columns), bf16),
            pltpu.SemaphoreType.DMA((len(spans(quads)),)),
        ],
        size=4 * prior.size,
        out_specs=HBM,
        limit=20,
    )(back)
    return jnp.transpose(out, (1, 0, 2))


def solution(mesh):
    placed = (
        P("mem", None, "reg"),
        P("mem", "reg", None),
        P("reg", None),
        P("reg", None),
        P("reg", "mem", None, None),
        P("reg", "mem", None),
    )
    return jax.shard_map(
        per_device, mesh=mesh, in_specs=placed, out_specs=P("mem", None, "reg"), check_vma=False
    )
```
